512 devices in a mesh: row: 32 (over y_lo, z), col: 16 (over y_hi, x, core).
Axes of the slice: x: 4, y: 8 (y_hi: 2, y_lo: 4; y = y_hi * 4 + y_lo), z: 8, core: 2. Of those that a mesh axis runs over, the one named last changes fastest.
Arguments:
- amplitudes: bfloat16 [640, 640, 2048], P('row', None, 'col'), may hold values from -6 to 6
- singles: bfloat16 [640, 200], P('col'), may hold values from -4 to 4
- integrals: bfloat16 [640, 640, 256], P('row', 'col'), may hold values from -0.0546875 to 0.0546875
- occ_energy: float32 [200], replicated, may hold values from -1 to -0.3
- pair_energy: float32 [256], P('row'), may hold values from 0.3 to 2
- occ_irrep: int32 [200], replicated, may hold values from 0 to 7, as said below
- virt_irrep: int32 [640], replicated, may hold values from 0 to 7, as said below
- pair_list: int32 [2048, 2], replicated, may hold values from 0 to 199, as said below
Outputs:
- update: bfloat16 [256, 2048], P('row', 'col')
The draws below stay inside these ranges and needn't reach their ends.
Inputs may be any that keep to these rules, and one draw needn't show every extreme that they name: `occ_irrep`: labels never fall along the orbital index and each of the eight labels occurs. `virt_irrep`: labels never fall along the orbital index and each of the eight labels occurs. `pair_list`: each row (i, j) has i <= j.
All inputs are finite; a program needn't handle non-finite values.
Results may differ from the reference program's by a relative error of at most 0.0049.
Values may be sent and summed in bfloat16 or wider, within the bound.
A program may use at most 64 MiB of HBM per device.

```python
import jax
import jax.numpy as jnp
from jax import lax

NO = 200
NV = 640
PAIRS = 2048
VPAIRS = 256


def sorted_labels(key, count):
    random_part = jax.random.randint(key, (count - 8,), 0, 8, dtype=jnp.int32)
    return jnp.sort(jnp.concatenate([jnp.arange(8, dtype=jnp.int32), random_part]))


def draw_occ_irrep(key, part):
    return sorted_labels(jax.random.fold_in(key, 11), NO)


def draw_virt_irrep(key, part):
    return sorted_labels(jax.random.fold_in(key, 12), NV)


def draw_pair_list(key, part):
    left_key = jax.random.fold_in(key, 21)
    right_key = jax.random.fold_in(key, 22)
    left_index = jax.random.randint(left_key, (PAIRS,), 0, NO, dtype=jnp.int32)
    right_index = jax.random.randint(right_key, (PAIRS,), 0, NO, dtype=jnp.int32)
    lower_index = jnp.minimum(left_index, right_index).at[0].set(0)
    upper_index = jnp.maximum(left_index, right_index).at[0].set(NO - 1)
    return jnp.stack([lower_index, upper_index], axis=1)


def strengthened(result, own_key, source, target, shards_of, factor):
    owner, partner = [(jnp.arange(result.shape[axis_at]) // (result.shape[axis_at] // shards_of)).reshape([-1 if axis == axis_at else 1 for axis in range(result.ndim)]) for axis_at in (source, target)]
    chosen = jax.random.permutation(own_key, shards_of)[partner]
    strong = (owner == chosen) | (owner == (partner + shards_of // 2) % shards_of)
    return jnp.where(strong, factor * result, result)


def steps_of(rng, dims, pieces, smallest, largest):
    def one(axis_at, shards_of):
        steps = jax.random.uniform(jax.random.fold_in(jax.random.fold_in(rng, 6), axis_at), (shards_of,), jnp.float32, smallest / len(pieces), largest / len(pieces))
        return jnp.repeat(jnp.exp(steps), dims[axis_at] // shards_of).reshape((-1,) + (1,) * (len(dims) - axis_at - 1))

    level = one(*pieces[0])
    for cut in pieces[1:]:
        level = level * one(*cut)
    return level


def noise(own_key, dims, deviation, limit, cuts=(), held_as=jnp.bfloat16):
    drawn = jax.random.normal(own_key, dims, jnp.float32) * deviation
    if len(cuts) > 0:
        drawn = steps_of(own_key, dims, cuts, -0.22, 0.18) * drawn
    return jnp.clip(drawn, min=-limit, max=limit).astype(held_as)


def heavy_noise(own_key, dims, spread, reach, cuts, heavy, kind=jnp.bfloat16):
    result = spread * jax.random.normal(own_key, dims, jnp.float32)
    if cuts:
        result = result * steps_of(own_key, dims, cuts, -0.22, 0.18)
    return jnp.clip(strengthened(result, jax.random.fold_in(own_key, 3), *heavy), -reach, reach).astype(kind)


def setup_inputs(seed: int = 0) -> dict:
    key_list = jax.random.split(jax.random.key(seed), 9)
    amplitudes = noise(key_list[0], (NV, NV, PAIRS), 1.0, 6.0, ((0, 32), (2, 16)))
    singles = noise(key_list[1], (NV, NO), 0.7, 4.0, ((0, 16),))
    integrals = heavy_noise(key_list[2], (NV, NV, VPAIRS), (NV * NV // 8) ** -0.5, 0.0546875, ((0, 32), (1, 16)), (0, 2, 32, 2.75))
    occ_energy = jnp.clip(jax.random.uniform(key_list[3], (NO,), jnp.float32, -1.0, -0.3), -1.0, -0.3)
    pair_energy = jnp.clip(0.3 + 1.7 * jax.random.uniform(key_list[4], (VPAIRS,), jnp.float32) ** steps_of(key_list[4], (VPAIRS,), ((0, 32),), -0.2, 0.2), 0.3, 2.0)
    occ_irrep = draw_occ_irrep(jax.random.fold_in(key_list[8], 71), 0)
    virt_irrep = draw_virt_irrep(jax.random.fold_in(key_list[8], 71), 0)
    pair_list = draw_pair_list(jax.random.fold_in(key_list[8], 71), 0)
    return {"amplitudes": amplitudes, "singles": singles, "integrals": integrals, "occ_energy": occ_energy, "pair_energy": pair_energy, "occ_irrep": occ_irrep, "virt_irrep": virt_irrep, "pair_list": pair_list}


def reference(amplitudes, singles, integrals, occ_energy, pair_energy, occ_irrep, virt_irrep, pair_list):
    first_occ = pair_list[:, 0].astype(jnp.int32)
    second_occ = pair_list[:, 1].astype(jnp.int32)
    pair_sym = jnp.bitwise_xor(occ_irrep[first_occ], occ_irrep[second_occ])
    d_terms = singles[:, second_occ].astype(jnp.float32)
    c_terms = singles[:, first_occ].astype(jnp.float32)

    def add_row(ladder_sum, row_items):
        amplitude_row, integral_row, c_single, c_label = row_items
        labels = jnp.bitwise_xor(jnp.bitwise_xor(virt_irrep[:, None], c_label), pair_sym[None, :])
        allowed = labels == 0
        value = amplitude_row.astype(jnp.float32) + c_single[None, :] * d_terms
        tau_block = jnp.where(allowed, value, jnp.zeros_like(value)).astype(jnp.bfloat16)
        contrib = jnp.dot(integral_row.T, tau_block, preferred_element_type=jnp.float32)
        return ladder_sum + contrib, None

    start_sum = jnp.zeros((VPAIRS, PAIRS), jnp.float32)
    ladder_sum, unused = lax.scan(add_row, start_sum, (amplitudes, integrals, c_terms, virt_irrep))
    denominator = pair_energy[:, None] - occ_energy[first_occ][None, :] - occ_energy[second_occ][None, :]
    return (ladder_sum / denominator).astype(jnp.bfloat16)
```

```python
import functools

import jax
import jax.numpy as jnp
from jax import lax
from jax.experimental import pallas as pl
from jax.experimental.pallas import tpu as pltpu
from jax.sharding import PartitionSpec as P

MESH = pl.DeviceIdType.MESH
NX = 4
ROWS = 32
COLS = 16
CORES = 2

CB = 20
DB = 40
KB = CB * DB
HB = KB // 2
NVIRT = 640
NOCC = 200
NPAIR = 128
NWIN = 256
NOUT = 8


def contract(a, b):
    return lax.dot_general(a, b, (((0,), (0,)), ((), ())), preferred_element_type=jnp.float32)


def kernel(
    amp_hbm, singles_hbm, integ_hbm, occ_e, pair_e, occ_l, virt_row, virt_l, pairs, out_ref,
    amp, sblk, ibuf, tau, labels, d_val, c_val, total, rbuf,
    local_sem, s_send, s_recv, send_sem, recv_sem, sib_send, sib_recv, r_send, r_recv,
):
    row = lax.axis_index("row")
    col = lax.axis_index("col")
    core = lax.rem(col, CORES)
    xat = lax.rem(col // CORES, NX)
    yhi = col // (CORES * NX)

    def col_of(y, x, k):
        return y * (CORES * NX) + x * CORES + k

    right = col_of(yhi, lax.rem(xat + 1, NX), core)
    left = col_of(yhi, lax.rem(xat + NX - 1, NX), core)
    across = col_of(1 - yhi, xat, core)
    sibling = col_of(yhi, xat, 1 - core)

    amp_copy = pltpu.make_async_copy(amp_hbm, amp, local_sem.at[0])
    amp_copy.start()
    own_copy = pltpu.make_async_copy(integ_hbm, ibuf.at[col], local_sem.at[1])
    own_copy.start()
    s_copy = pltpu.make_async_copy(singles_hbm, sblk.at[col], local_sem.at[2])
    s_copy.start()

    barrier = pltpu.get_barrier_semaphore()

    def greet_row(step, carry):
        other = lax.rem(row + step, ROWS)
        pl.semaphore_signal(barrier, inc=1, device_id=(other, col), device_id_type=MESH)
        return carry

    def greet_col(step, carry):
        other = lax.rem(col + step, COLS)
        pl.semaphore_signal(barrier, inc=1, device_id=(row, other), device_id_type=MESH)
        return carry

    lax.fori_loop(1, COLS, greet_col, 0)
    lax.fori_loop(1, ROWS, greet_row, 0)
    pl.semaphore_wait(barrier, ROWS - 1 + COLS - 1)

    def send_single(step, carry):
        other = lax.rem(col + step, COLS)
        pltpu.make_async_remote_copy(
            src_ref=singles_hbm, dst_ref=sblk.at[col], send_sem=s_send.at[0], recv_sem=s_recv.at[0],
            device_id=(row, other), device_id_type=MESH,
        ).start()
        return carry

    lax.fori_loop(1, COLS, send_single, 0)

    started = []

    def half(at, h):
        return ibuf.at[at, pl.ds(h * HB, HB)]

    def push(src, at, h, target, slot):
        copy = pltpu.make_async_remote_copy(
            src_ref=src, dst_ref=half(at, h), send_sem=send_sem.at[len(started)], recv_sem=recv_sem.at[slot],
            device_id=(row, target), device_id_type=MESH,
        )
        copy.start()
        started.append(copy)

    def to_sibling(src, at, h, slot):
        copy = pltpu.make_async_remote_copy(
            src_ref=src, dst_ref=half(at, h), send_sem=sib_send.at[slot], recv_sem=sib_recv.at[slot],
            device_id=(row, sibling), device_id_type=MESH,
        )
        copy.start()
        sib_started.append(copy)

    sib_started = []

    def arrived(at, h, slot):
        ref = half(at, h)
        pltpu.make_async_copy(ref, ref, recv_sem.at[slot]).wait()

    def sib_arrived(at, h, slot):
        ref = half(at, h)
        pltpu.make_async_copy(ref, ref, sib_recv.at[slot]).wait()

    def slot_of(s, q, h):
        return (s * 4 + q) * 2 + h

    def block_of(s, q, k):
        y = yhi if s == 0 else 1 - yhi
        x = lax.rem(xat + (0, NX - 1, 1, 2)[q], NX)
        return col_of(y, x, k)

    def own_half(h):
        return integ_hbm.at[pl.ds(h * HB, HB)]

    push(own_half(0), col, 0, across, slot_of(1, 0, 0))
    push(own_half(0), col, 0, right, slot_of(0, 1, 0))
    push(own_half(1), col, 1, left, slot_of(0, 2, 1))
    push(own_half(1), col, 1, across, slot_of(1, 0, 1))
    push(own_half(1), col, 1, right, slot_of(0, 1, 1))
    push(own_half(0), col, 0, left, slot_of(0, 2, 0))
    for h in range(2):
        to_sibling(own_half(h), col, h, slot_of(0, 0, h))

    first = pairs[0:1, pl.ds(pl.multiple_of(col * NPAIR, NPAIR), NPAIR)]
    second = pairs[1:2, pl.ds(pl.multiple_of(col * NPAIR, NPAIR), NPAIR)]
    both = jnp.concatenate([second, first], axis=1)
    orbital = lax.broadcasted_iota(jnp.int32, (NOCC, 2 * NPAIR), 0)
    pick = jnp.where(orbital == both, 1.0, 0.0).astype(jnp.bfloat16)

    energy = occ_e[...]
    part_a = energy.astype(jnp.bfloat16).astype(jnp.float32)
    part_b = (energy - part_a).astype(jnp.bfloat16).astype(jnp.float32)
    part_c = energy - part_a - part_b
    place = lax.broadcasted_iota(jnp.int32, (16, NOCC), 0)
    table = jnp.where(place == 0, part_a, jnp.where(place == 1, part_b, jnp.where(place == 2, part_c, 0.0)))
    table = jnp.where(place == 3, occ_l[...].astype(jnp.float32), table).astype(jnp.bfloat16)
    found = jnp.dot(table, pick, preferred_element_type=jnp.float32)
    occ_pair = found[0:1] + found[1:2] + found[2:3]
    label_pair = found[3:4].astype(jnp.int32)
    e_second, e_first = occ_pair[:, :NPAIR], occ_pair[:, NPAIR:]
    sym = jnp.bitwise_xor(label_pair[:, :NPAIR], label_pair[:, NPAIR:])
    virt = jnp.broadcast_to(virt_row[...].astype(jnp.float32), (NPAIR, NVIRT)).T
    labels[...] = jnp.bitwise_xor(virt.astype(jnp.int32), sym)
    total[...] = jnp.zeros_like(total)

    s_copy.wait()
    others = sblk.at[pl.ds(0, COLS - 1)]
    pltpu.make_async_copy(others, others, s_recv.at[0]).wait()
    for b in range(COLS):
        at_pairs = jnp.dot(sblk[b], pick, preferred_element_type=jnp.float32)
        d_val[pl.ds(b * DB, DB), :] = at_pairs[:, :NPAIR]
        c_val[pl.ds(b * DB, DB), :] = at_pairs[:, NPAIR:]
    amp_copy.wait()

    def tau_step(m, carry):
        d_at = pl.multiple_of(m * (2 * DB), 2 * DB)
        d_lab = labels[pl.ds(d_at, 2 * DB), :]
        d_one = d_val[pl.ds(d_at, 2 * DB), :]

        def tau_pair(c2, carry):
            vals = []
            for u in range(2):
                c = c2 * 2 + u
                c_one = c_val[pl.ds(row * CB + c, 1), :]
                val = amp[c, pl.ds(d_at, 2 * DB), :].astype(jnp.float32) + c_one * d_one
                vals.append(jnp.where(d_lab == virt_l[row * CB + c], val, 0.0))
            k_at = pl.multiple_of(c2 * (2 * DB), 2 * DB)
            for v in range(2):
                rows = jnp.concatenate([val[v * DB : (v + 1) * DB] for val in vals], axis=0)
                tau[m * 2 + v, pl.ds(k_at, 2 * DB), :] = rows.astype(jnp.bfloat16)
            return carry

        return lax.fori_loop(0, CB // 2, tau_pair, carry)

    lax.fori_loop(0, COLS // 2, tau_step, 0)

    def add_block(at):
        total[...] += contract(ibuf[at], tau[at])

    def pass_on(s, q, h, onward=()):
        at = block_of(s, q, core)
        arrived(at, h, slot_of(s, q, h))
        for target, q_there in onward:
            push(half(at, h), at, h, target, slot_of(s, q_there, h))
        to_sibling(half(at, h), at, h, slot_of(s, q, h))

    def add_sibling(s, q):
        at = block_of(s, q, 1 - core)
        for h in range(2):
            sib_arrived(at, h, slot_of(s, q, h))
        add_block(at)

    pass_on(0, 1, 0, [(right, 3)])
    pass_on(0, 2, 1, [(left, 3)])
    own_copy.wait()
    add_block(col)
    pass_on(1, 0, 0, [(right, 1), (left, 2)])
    pass_on(0, 1, 1)
    pass_on(0, 2, 0)
    add_sibling(0, 0)
    add_block(block_of(0, 1, core))
    pass_on(0, 3, 0)
    pass_on(0, 3, 1)
    pass_on(1, 0, 1, [(left, 2), (right, 1)])
    add_block(block_of(0, 2, core))
    add_block(block_of(0, 3, core))
    pass_on(1, 1, 0, [(right, 3)])
    add_sibling(0, 1)
    add_sibling(0, 2)
    pass_on(1, 2, 0)
    pass_on(1, 2, 1, [(left, 3)])
    add_block(block_of(1, 0, core))
    add_sibling(0, 3)
    pass_on(1, 1, 1)
    add_block(block_of(1, 1, core))
    add_block(block_of(1, 2, core))
    add_sibling(1, 0)
    pass_on(1, 3, 0)
    pass_on(1, 3, 1)
    add_sibling(1, 1)
    add_sibling(1, 2)
    add_block(block_of(1, 3, core))
    add_sibling(1, 3)

    def send_rows(step, carry):
        other = lax.rem(row + step, ROWS)
        pltpu.make_async_remote_copy(
            src_ref=total.at[pl.ds(pl.multiple_of(other * NOUT, NOUT), NOUT)], dst_ref=rbuf.at[row],
            send_sem=r_send.at[0], recv_sem=r_recv.at[0], device_id=(other, col), device_id_type=MESH,
        ).start()
        return carry

    lax.fori_loop(1, ROWS, send_rows, 0)
    rbuf[row] = total[pl.ds(pl.multiple_of(row * NOUT, NOUT), NOUT), :]
    at_row = lax.broadcasted_iota(jnp.int32, (NOUT, NPAIR), 0)
    window = jnp.zeros((NOUT, NPAIR), jnp.float32)
    for n in range(NOUT):
        window = jnp.where(at_row == n, pair_e[n], window)
    denominator = window - e_first - e_second
    peers = rbuf.at[pl.ds(0, ROWS - 1)]
    pltpu.make_async_copy(peers, peers, r_recv.at[0]).wait()
    ladder = rbuf[0]
    for r in range(1, ROWS):
        ladder = ladder + rbuf[r]
    out_ref[...] = (ladder / denominator).astype(jnp.bfloat16)

    for copy in started + sib_started:
        copy.wait_send()
    pltpu.make_async_copy(others, others, s_send.at[0]).wait()
    pltpu.make_async_copy(peers, peers, r_send.at[0]).wait()


def body(amplitudes, singles, integrals, occ_energy, pair_energy, occ_irrep, virt_irrep, pair_list):
    hbm = pl.BlockSpec(memory_space=pltpu.MemorySpace.HBM)
    vmem = pl.BlockSpec(memory_space=pltpu.VMEM)
    smem = pl.BlockSpec(memory_space=pltpu.SMEM)
    dma = pltpu.SemaphoreType.DMA
    return pl.pallas_call(
        kernel,
        out_shape=jax.ShapeDtypeStruct((NOUT, NPAIR), jnp.bfloat16),
        in_specs=[hbm, hbm, hbm, vmem, smem, vmem, vmem, smem, vmem],
        out_specs=vmem,
        scratch_shapes=[
            pltpu.VMEM((CB, NVIRT, NPAIR), jnp.bfloat16),
            pltpu.VMEM((COLS, DB, NOCC), jnp.bfloat16),
            pltpu.VMEM((COLS, KB, NWIN), jnp.bfloat16),
            pltpu.VMEM((COLS, KB, NPAIR), jnp.bfloat16),
            pltpu.VMEM((NVIRT, NPAIR), jnp.int32),
            pltpu.VMEM((NVIRT, NPAIR), jnp.float32),
            pltpu.VMEM((NVIRT, NPAIR), jnp.float32),
            pltpu.VMEM((NWIN, NPAIR), jnp.float32),
            pltpu.VMEM((ROWS, NOUT, NPAIR), jnp.float32),
            dma((3,)),
            dma((1,)),
            dma((1,)),
            dma((14,)),
            dma((16,)),
            dma((16,)),
            dma((16,)),
            dma((1,)),
            dma((1,)),
        ],
        compiler_params=pltpu.CompilerParams(
            collective_id=0, has_side_effects=True, vmem_limit_bytes=48 * 1024 * 1024
        ),
        name="ladder",
    )(
        amplitudes,
        singles,
        integrals.reshape(KB, NWIN),
        occ_energy.reshape(1, NOCC),
        pair_energy,
        occ_irrep.reshape(1, NOCC),
        virt_irrep.reshape(1, NVIRT),
        virt_irrep,
        pair_list.T,
    )


def solution(mesh):
    return jax.shard_map(
        body,
        mesh=mesh,
        in_specs=(
            P("row", None, "col"),
            P("col", None),
            P("row", "col", None),
            P(),
            P("row"),
            P(),
            P(),
            P(),
        ),
        out_specs=P("row", "col"),
        check_vma=False,
    )
```

```python
import functools

import jax
import jax.numpy as jnp
from jax import lax
from jax.experimental import pallas as pl
from jax.experimental.pallas import tpu as pltpu
from jax.sharding import PartitionSpec as P

MESH = pl.DeviceIdType.MESH
NX = 4
ROWS = 32
COLS = 16
CORES = 2

CB = 20
DB = 40
KB = CB * DB
HB = KB // 2
NVIRT = 640
NOCC = 200
NPAIR = 128
NWIN = 256
NOUT = 8


def contract(a, b):
    return lax.dot_general(a, b, (((0,), (0,)), ((), ())), preferred_element_type=jnp.float32)


def kernel(
    amp_hbm, singles_hbm, integ_hbm, occ_e_hbm, pair_e_hbm, occ_l_hbm, virt_hbm, pairs_hbm, out_ref,
    occ_e, pair_e, occ_l, virt_row, virt_l, pairs, amp, sblk, ibuf, tau, labels, d_val, c_val, total, rbuf,
    local_sem, s_send, s_recv, send_sem, recv_sem, sib_send, sib_recv, r_send, r_recv,
):
    row = lax.axis_index("row")
    col = lax.axis_index("col")
    core = lax.rem(col, CORES)
    xat = lax.rem(col // CORES, NX)
    yhi = col // (CORES * NX)

    def col_of(y, x, k):
        return y * (CORES * NX) + x * CORES + k

    right = col_of(yhi, lax.rem(xat + 1, NX), core)
    left = col_of(yhi, lax.rem(xat + NX - 1, NX), core)
    across = col_of(1 - yhi, xat, core)
    sibling = col_of(yhi, xat, 1 - core)

    amp_copy = pltpu.make_async_copy(amp_hbm, amp, local_sem.at[0])
    amp_copy.start()
    own_copy = pltpu.make_async_copy(integ_hbm, ibuf.at[col], local_sem.at[1])
    own_copy.start()
    s_copy = pltpu.make_async_copy(singles_hbm, sblk.at[col], local_sem.at[2])
    s_copy.start()

    small_copies = []
    for n, (src, dst) in enumerate(
        (
            (pairs_hbm, pairs),
            (occ_e_hbm, occ_e),
            (occ_l_hbm, occ_l),
            (virt_hbm, virt_row),
            (virt_hbm, virt_l),
            (pair_e_hbm, pair_e),
        )
    ):
        copy = pltpu.make_async_copy(src, dst, local_sem.at[3 + n])
        copy.start()
        small_copies.append(copy)

    barrier = pltpu.get_barrier_semaphore()

    def greet_row(step, carry):
        other = lax.rem(row + step, ROWS)
        pl.semaphore_signal(barrier, inc=1, device_id=(other, col), device_id_type=MESH)
        return carry

    def greet_col(step, carry):
        other = lax.rem(col + step, COLS)
        pl.semaphore_signal(barrier, inc=1, device_id=(row, other), device_id_type=MESH)
        return carry

    lax.fori_loop(1, COLS, greet_col, 0)
    lax.fori_loop(1, ROWS, greet_row, 0)
    pl.semaphore_wait(barrier, ROWS - 1 + COLS - 1)

    def send_single(step, carry):
        other = lax.rem(col + step, COLS)
        pltpu.make_async_remote_copy(
            src_ref=singles_hbm, dst_ref=sblk.at[col], send_sem=s_send.at[0], recv_sem=s_recv.at[0],
            device_id=(row, other), device_id_type=MESH,
        ).start()
        return carry

    lax.fori_loop(1, COLS, send_single, 0)

    started = []

    def half(at, h):
        return ibuf.at[at, pl.ds(h * HB, HB)]

    def push(src, at, h, target, slot):
        copy = pltpu.make_async_remote_copy(
            src_ref=src, dst_ref=half(at, h), send_sem=send_sem.at[len(started)], recv_sem=recv_sem.at[slot],
            device_id=(row, target), device_id_type=MESH,
        )
        copy.start()
        started.append(copy)

    def to_sibling(src, at, h, slot):
        copy = pltpu.make_async_remote_copy(
            src_ref=src, dst_ref=half(at, h), send_sem=sib_send.at[slot], recv_sem=sib_recv.at[slot],
            device_id=(row, sibling), device_id_type=MESH,
        )
        copy.start()
        sib_started.append(copy)

    sib_started = []

    def arrived(at, h, slot):
        ref = half(at, h)
        pltpu.make_async_copy(ref, ref, recv_sem.at[slot]).wait()

    def sib_arrived(at, h, slot):
        ref = half(at, h)
        pltpu.make_async_copy(ref, ref, sib_recv.at[slot]).wait()

    def slot_of(s, q, h):
        return (s * 4 + q) * 2 + h

    def block_of(s, q, k):
        y = yhi if s == 0 else 1 - yhi
        x = lax.rem(xat + (0, NX - 1, 1, 2)[q], NX)
        return col_of(y, x, k)

    def own_half(h):
        return integ_hbm.at[pl.ds(h * HB, HB)]

    push(own_half(0), col, 0, across, slot_of(1, 0, 0))
    push(own_half(0), col, 0, right, slot_of(0, 1, 0))
    push(own_half(1), col, 1, left, slot_of(0, 2, 1))
    push(own_half(1), col, 1, across, slot_of(1, 0, 1))
    push(own_half(1), col, 1, right, slot_of(0, 1, 1))
    push(own_half(0), col, 0, left, slot_of(0, 2, 0))
    for h in range(2):
        to_sibling(own_half(h), col, h, slot_of(0, 0, h))

    for copy in small_copies:
        copy.wait()
    first = pairs[0:1, pl.ds(pl.multiple_of(col * NPAIR, NPAIR), NPAIR)]
    second = pairs[1:2, pl.ds(pl.multiple_of(col * NPAIR, NPAIR), NPAIR)]
    both = jnp.concatenate([second, first], axis=1)
    orbital = lax.broadcasted_iota(jnp.int32, (NOCC, 2 * NPAIR), 0)
    pick = jnp.where(orbital == both, 1.0, 0.0).astype(jnp.bfloat16)

    energy = occ_e[...]
    part_a = energy.astype(jnp.bfloat16).astype(jnp.float32)
    part_b = (energy - part_a).astype(jnp.bfloat16).astype(jnp.float32)
    part_c = energy - part_a - part_b
    place = lax.broadcasted_iota(jnp.int32, (16, NOCC), 0)
    table = jnp.where(place == 0, part_a, jnp.where(place == 1, part_b, jnp.where(place == 2, part_c, 0.0)))
    table = jnp.where(place == 3, occ_l[...].astype(jnp.float32), table).astype(jnp.bfloat16)
    found = jnp.dot(table, pick, preferred_element_type=jnp.float32)
    occ_pair = found[0:1] + found[1:2] + found[2:3]
    label_pair = found[3:4].astype(jnp.int32)
    e_second, e_first = occ_pair[:, :NPAIR], occ_pair[:, NPAIR:]
    sym = jnp.bitwise_xor(label_pair[:, :NPAIR], label_pair[:, NPAIR:])
    virt = jnp.broadcast_to(virt_row[...].reshape(1, NVIRT).astype(jnp.float32), (NPAIR, NVIRT)).T
    labels[...] = jnp.bitwise_xor(virt.astype(jnp.int32), sym)
    total[...] = jnp.zeros_like(total)

    s_copy.wait()
    others = sblk.at[pl.ds(0, COLS - 1)]
    pltpu.make_async_copy(others, others, s_recv.at[0]).wait()
    for b in range(COLS):
        at_pairs = jnp.dot(sblk[b], pick, preferred_element_type=jnp.float32)
        d_val[pl.ds(b * DB, DB), :] = at_pairs[:, :NPAIR]
        c_val[pl.ds(b * DB, DB), :] = at_pairs[:, NPAIR:]
    amp_copy.wait()

    def tau_step(m, carry):
        d_at = pl.multiple_of(m * (2 * DB), 2 * DB)
        d_lab = labels[pl.ds(d_at, 2 * DB), :]
        d_one = d_val[pl.ds(d_at, 2 * DB), :]

        def tau_pair(c2, carry):
            vals = []
            for u in range(2):
                c = c2 * 2 + u
                c_one = c_val[pl.ds(row * CB + c, 1), :]
                val = amp[c, pl.ds(d_at, 2 * DB), :].astype(jnp.float32) + c_one * d_one
                vals.append(jnp.where(d_lab == virt_l[row * CB + c], val, 0.0))
            k_at = pl.multiple_of(c2 * (2 * DB), 2 * DB)
            for v in range(2):
                rows = jnp.concatenate([val[v * DB : (v + 1) * DB] for val in vals], axis=0)
                tau[m * 2 + v, pl.ds(k_at, 2 * DB), :] = rows.astype(jnp.bfloat16)
            return carry

        return lax.fori_loop(0, CB // 2, tau_pair, carry)

    lax.fori_loop(0, COLS // 2, tau_step, 0)

    def add_block(at):
        total[...] += contract(ibuf[at], tau[at])

    def pass_on(s, q, h, onward=()):
        at = block_of(s, q, core)
        arrived(at, h, slot_of(s, q, h))
        for target, q_there in onward:
            push(half(at, h), at, h, target, slot_of(s, q_there, h))
        to_sibling(half(at, h), at, h, slot_of(s, q, h))

    def add_sibling(s, q):
        at = block_of(s, q, 1 - core)
        for h in range(2):
            sib_arrived(at, h, slot_of(s, q, h))
        add_block(at)

    pass_on(0, 1, 0, [(right, 3)])
    pass_on(0, 2, 1, [(left, 3)])
    own_copy.wait()
    add_block(col)
    pass_on(1, 0, 0, [(right, 1), (left, 2)])
    pass_on(0, 1, 1)
    pass_on(0, 2, 0)
    add_sibling(0, 0)
    add_block(block_of(0, 1, core))
    pass_on(0, 3, 0)
    pass_on(0, 3, 1)
    pass_on(1, 0, 1, [(left, 2), (right, 1)])
    add_block(block_of(0, 2, core))
    add_block(block_of(0, 3, core))
    pass_on(1, 1, 0, [(right, 3)])
    add_sibling(0, 1)
    add_sibling(0, 2)
    pass_on(1, 2, 0)
    pass_on(1, 2, 1, [(left, 3)])
    add_block(block_of(1, 0, core))
    add_sibling(0, 3)
    pass_on(1, 1, 1)
    add_block(block_of(1, 1, core))
    add_block(block_of(1, 2, core))
    add_sibling(1, 0)
    pass_on(1, 3, 0)
    pass_on(1, 3, 1)
    add_sibling(1, 1)
    add_sibling(1, 2)
    add_block(block_of(1, 3, core))
    add_sibling(1, 3)

    def send_rows(step, carry):
        other = lax.rem(row + step, ROWS)
        pltpu.make_async_remote_copy(
            src_ref=total.at[pl.ds(pl.multiple_of(other * NOUT, NOUT), NOUT)], dst_ref=rbuf.at[row],
            send_sem=r_send.at[0], recv_sem=r_recv.at[0], device_id=(other, col), device_id_type=MESH,
        ).start()
        return carry

    lax.fori_loop(1, ROWS, send_rows, 0)
    rbuf[row] = total[pl.ds(pl.multiple_of(row * NOUT, NOUT), NOUT), :]
    at_row = lax.broadcasted_iota(jnp.int32, (NOUT, NPAIR), 0)
    window = jnp.zeros((NOUT, NPAIR), jnp.float32)
    for n in range(NOUT):
        window = jnp.where(at_row == n, pair_e[n], window)
    denominator = window - e_first - e_second
    peers = rbuf.at[pl.ds(0, ROWS - 1)]
    pltpu.make_async_copy(peers, peers, r_recv.at[0]).wait()
    ladder = rbuf[0]
    for r in range(1, ROWS):
        ladder = ladder + rbuf[r]
    out_ref[...] = (ladder / denominator).astype(jnp.bfloat16)

    for copy in started + sib_started:
        copy.wait_send()
    pltpu.make_async_copy(others, others, s_send.at[0]).wait()
    pltpu.make_async_copy(peers, peers, r_send.at[0]).wait()


def body(amplitudes, singles, integrals, occ_energy, pair_energy, occ_irrep, virt_irrep, pair_list):
    hbm = pl.BlockSpec(memory_space=pltpu.MemorySpace.HBM)
    vmem = pl.BlockSpec(memory_space=pltpu.VMEM)
    dma = pltpu.SemaphoreType.DMA
    return pl.pallas_call(
        kernel,
        out_shape=jax.ShapeDtypeStruct((NOUT, NPAIR), jnp.bfloat16),
        in_specs=[hbm] * 8,
        out_specs=vmem,
        scratch_shapes=[
            pltpu.VMEM((1, NOCC), jnp.float32),
            pltpu.SMEM((NOUT,), jnp.float32),
            pltpu.VMEM((1, NOCC), jnp.int32),
            pltpu.VMEM((NVIRT,), jnp.int32),
            pltpu.SMEM((NVIRT,), jnp.int32),
            pltpu.VMEM((2, COLS * NPAIR), jnp.int32),
            pltpu.VMEM((CB, NVIRT, NPAIR), jnp.bfloat16),
            pltpu.VMEM((COLS, DB, NOCC), jnp.bfloat16),
            pltpu.VMEM((COLS, KB, NWIN), jnp.bfloat16),
            pltpu.VMEM((COLS, KB, NPAIR), jnp.bfloat16),
            pltpu.VMEM((NVIRT, NPAIR), jnp.int32),
            pltpu.VMEM((NVIRT, NPAIR), jnp.float32),
            pltpu.VMEM((NVIRT, NPAIR), jnp.float32),
            pltpu.VMEM((NWIN, NPAIR), jnp.float32),
            pltpu.VMEM((ROWS, NOUT, NPAIR), jnp.float32),
            dma((9,)),
            dma((1,)),
            dma((1,)),
            dma((14,)),
            dma((16,)),
            dma((16,)),
            dma((16,)),
            dma((1,)),
            dma((1,)),
        ],
        compiler_params=pltpu.CompilerParams(
            collective_id=0, has_side_effects=True, vmem_limit_bytes=67043328
        ),
        name="ladder",
    )(
        amplitudes,
        singles,
        integrals.reshape(KB, NWIN),
        occ_energy.reshape(1, NOCC),
        pair_energy,
        occ_irrep.reshape(1, NOCC),
        virt_irrep,
        pair_list.T,
    )


def solution(mesh):
    return jax.shard_map(
        body,
        mesh=mesh,
        in_specs=(
            P("row", None, "col"),
            P("col", None),
            P("row", "col", None),
            P(),
            P("row"),
            P(),
            P(),
            P(),
        ),
        out_specs=P("row", "col"),
        check_vma=False,
    )
```

```python
import functools

import jax
import jax.numpy as jnp
from jax import lax
from jax.experimental import pallas as pl
from jax.experimental.pallas import tpu as pltpu
from jax.sharding import PartitionSpec as P

MESH = pl.DeviceIdType.MESH
NX = 4
ROWS = 32
COLS = 16
CORES = 2

CB = 20
DB = 40
KB = CB * DB
PIECES = ((0, 208), (208, 192), (400, 208), (608, 192))
PLANE = 8
NVIRT = 640
NOCC = 200
NPAIR = 128
NWIN = 256
NOUT = 8


def contract(a, b):
    return lax.dot_general(a, b, (((0,), (0,)), ((), ())), preferred_element_type=jnp.float32)


def kernel(
    amp_hbm, singles_hbm, integ_hbm, occ_e_hbm, pair_e_hbm, occ_l_hbm, virt_hbm, pairs_hbm, out_ref,
    occ_e, pair_e, occ_l, virt_row, virt_l, pairs, amp, sblk, ibuf, tau, labels, d_val, c_val, total, rbuf,
    local_sem, s_send, s_recv, send_sem, recv_sem, sib_send, sib_recv, r_send, r_recv,
):
    row = lax.axis_index("row")
    col = lax.axis_index("col")
    core = lax.rem(col, CORES)
    xat = lax.rem(col // CORES, NX)
    yhi = col // (CORES * NX)

    def col_of(y, x, k):
        return y * (CORES * NX) + x * CORES + k

    right = col_of(yhi, lax.rem(xat + 1, NX), core)
    left = col_of(yhi, lax.rem(xat + NX - 1, NX), core)
    across = col_of(1 - yhi, xat, core)
    sibling = col_of(yhi, xat, 1 - core)

    amp_copy = pltpu.make_async_copy(amp_hbm, amp, local_sem.at[0])
    amp_copy.start()
    own_copy = pltpu.make_async_copy(integ_hbm, ibuf.at[col], local_sem.at[1])
    own_copy.start()
    spot = col // CORES
    s_copy = pltpu.make_async_copy(singles_hbm, sblk.at[core, spot], local_sem.at[2])
    s_copy.start()

    small_copies = []
    for n, (src, dst) in enumerate(
        (
            (pairs_hbm, pairs),
            (occ_e_hbm, occ_e),
            (occ_l_hbm, occ_l),
            (virt_hbm, virt_row),
            (virt_hbm, virt_l),
            (pair_e_hbm, pair_e),
        )
    ):
        copy = pltpu.make_async_copy(src, dst, local_sem.at[3 + n])
        copy.start()
        small_copies.append(copy)

    barrier = pltpu.get_barrier_semaphore()

    def greet_row(step, carry):
        other = lax.rem(row + step, ROWS)
        pl.semaphore_signal(barrier, inc=1, device_id=(other, col), device_id_type=MESH)
        return carry

    def greet_plane(step, carry):
        other = lax.rem(spot + step, PLANE) * CORES + core
        pl.semaphore_signal(barrier, inc=1, device_id=(row, other), device_id_type=MESH)
        return carry

    pl.semaphore_signal(barrier, inc=1, device_id=(row, sibling), device_id_type=MESH)
    lax.fori_loop(1, PLANE, greet_plane, 0)
    lax.fori_loop(1, ROWS, greet_row, 0)
    pl.semaphore_wait(barrier, ROWS - 1 + PLANE)

    def send_single(step, carry):
        other = lax.rem(spot + step, PLANE) * CORES + core
        pltpu.make_async_remote_copy(
            src_ref=singles_hbm, dst_ref=sblk.at[core, spot], send_sem=s_send.at[0], recv_sem=s_recv.at[0],
            device_id=(row, other), device_id_type=MESH,
        ).start()
        return carry

    lax.fori_loop(1, PLANE, send_single, 0)

    started = []

    def half(at, h):
        return ibuf.at[at, pl.ds(*PIECES[h])]

    def push(src, at, h, target, slot):
        copy = pltpu.make_async_remote_copy(
            src_ref=src, dst_ref=half(at, h), send_sem=send_sem.at[len(started)], recv_sem=recv_sem.at[slot],
            device_id=(row, target), device_id_type=MESH,
        )
        copy.start()
        started.append(copy)

    def to_sibling(src, at, h, slot):
        copy = pltpu.make_async_remote_copy(
            src_ref=src, dst_ref=half(at, h), send_sem=sib_send.at[slot], recv_sem=sib_recv.at[slot],
            device_id=(row, sibling), device_id_type=MESH,
        )
        copy.start()
        sib_started.append(copy)

    sib_started = []

    def arrived(at, h, slot):
        ref = half(at, h)
        pltpu.make_async_copy(ref, ref, recv_sem.at[slot]).wait()

    def sib_arrived(at, h, slot):
        ref = half(at, h)
        pltpu.make_async_copy(ref, ref, sib_recv.at[slot]).wait()

    def slot_of(s, q, h):
        return (s * 4 + q) * len(PIECES) + h

    def block_of(s, q, k):
        y = yhi if s == 0 else 1 - yhi
        x = lax.rem(xat + (0, NX - 1, 1, 2)[q], NX)
        return col_of(y, x, k)

    def own_half(h):
        return integ_hbm.at[pl.ds(*PIECES[h])]

    for to_right, to_left, to_across in ((0, 2, 0), (1, 3, 2), (2, 0, 1), (3, 1, 3)):
        push(own_half(to_across), col, to_across, across, slot_of(1, 0, to_across))
        push(own_half(to_right), col, to_right, right, slot_of(0, 1, to_right))
        push(own_half(to_left), col, to_left, left, slot_of(0, 2, to_left))
    for h in range(len(PIECES)):
        to_sibling(own_half(h), col, h, slot_of(0, 0, h))

    for copy in small_copies:
        copy.wait()
    first = pairs[0:1, pl.ds(pl.multiple_of(col * NPAIR, NPAIR), NPAIR)]
    second = pairs[1:2, pl.ds(pl.multiple_of(col * NPAIR, NPAIR), NPAIR)]
    both = jnp.concatenate([second, first], axis=1)
    orbital = lax.broadcasted_iota(jnp.int32, (NOCC, 2 * NPAIR), 0)
    pick = jnp.where(orbital == both, 1.0, 0.0).astype(jnp.bfloat16)

    energy = occ_e[...]
    part_a = energy.astype(jnp.bfloat16).astype(jnp.float32)
    part_b = (energy - part_a).astype(jnp.bfloat16).astype(jnp.float32)
    part_c = energy - part_a - part_b
    place = lax.broadcasted_iota(jnp.int32, (16, NOCC), 0)
    table = jnp.where(place == 0, part_a, jnp.where(place == 1, part_b, jnp.where(place == 2, part_c, 0.0)))
    table = jnp.where(place == 3, occ_l[...].astype(jnp.float32), table).astype(jnp.bfloat16)
    found = jnp.dot(table, pick, preferred_element_type=jnp.float32)
    occ_pair = found[0:1] + found[1:2] + found[2:3]
    label_pair = found[3:4].astype(jnp.int32)
    e_second, e_first = occ_pair[:, :NPAIR], occ_pair[:, NPAIR:]
    sym = jnp.bitwise_xor(label_pair[:, :NPAIR], label_pair[:, NPAIR:])
    virt = jnp.broadcast_to(virt_row[...].reshape(1, NVIRT).astype(jnp.float32), (NPAIR, NVIRT)).T
    labels[...] = jnp.bitwise_xor(virt.astype(jnp.int32), sym)
    total[...] = jnp.zeros_like(total)

    def add_block(at):
        total[...] += contract(ibuf[at], tau[at])

    def pass_on(s, q, h, onward=()):
        at = block_of(s, q, core)
        arrived(at, h, slot_of(s, q, h))
        for target, q_there in onward:
            push(half(at, h), at, h, target, slot_of(s, q_there, h))
        to_sibling(half(at, h), at, h, slot_of(s, q, h))

    def add_sibling(s, q):
        at = block_of(s, q, 1 - core)
        for h in range(len(PIECES)):
            sib_arrived(at, h, slot_of(s, q, h))
        add_block(at)

    pass_on(0, 1, 0, [(right, 3)])
    pass_on(0, 2, 2, [(left, 3)])
    s_copy.wait()
    others = sblk.at[0, pl.ds(0, PLANE - 1)]
    pltpu.make_async_copy(others, others, s_recv.at[0]).wait()
    plane_copy = pltpu.make_async_remote_copy(
        src_ref=sblk.at[core], dst_ref=sblk.at[core], send_sem=s_send.at[1], recv_sem=s_recv.at[1],
        device_id=(row, sibling), device_id_type=MESH,
    )
    plane_copy.start()
    pass_on(0, 1, 1, [(right, 3)])
    pass_on(0, 2, 3, [(left, 3)])
    plane_copy.wait_recv()
    for b in range(COLS):
        at_pairs = jnp.dot(sblk[b % CORES, b // CORES], pick, preferred_element_type=jnp.float32)
        d_val[pl.ds(b * DB, DB), :] = at_pairs[:, :NPAIR]
        c_val[pl.ds(b * DB, DB), :] = at_pairs[:, NPAIR:]
    amp_copy.wait()

    def tau_step(m, carry):
        d_at = pl.multiple_of(m * (2 * DB), 2 * DB)
        d_lab = labels[pl.ds(d_at, 2 * DB), :]
        d_one = d_val[pl.ds(d_at, 2 * DB), :]

        def tau_pair(c2, carry):
            vals = []
            for u in range(2):
                c = c2 * 2 + u
                c_one = c_val[pl.ds(row * CB + c, 1), :]
                val = amp[c, pl.ds(d_at, 2 * DB), :].astype(jnp.float32) + c_one * d_one
                vals.append(jnp.where(d_lab == virt_l[row * CB + c], val, 0.0))
            k_at = pl.multiple_of(c2 * (2 * DB), 2 * DB)
            for v in range(2):
                rows = jnp.concatenate([val[v * DB : (v + 1) * DB] for val in vals], axis=0)
                tau[m * 2 + v, pl.ds(k_at, 2 * DB), :] = rows.astype(jnp.bfloat16)
            return carry

        return lax.fori_loop(0, CB // 2, tau_pair, carry)

    lax.fori_loop(0, COLS // 2, tau_step, 0)

    pass_on(1, 0, 0, [(right, 1), (left, 2)])
    pass_on(0, 1, 2)
    pass_on(0, 2, 0)
    own_copy.wait()
    add_block(col)
    pass_on(0, 1, 3)
    pass_on(0, 2, 1)
    pass_on(1, 0, 2, [(left, 2), (right, 1)])
    add_sibling(0, 0)
    add_block(block_of(0, 1, core))
    pass_on(0, 3, 0)
    pass_on(0, 3, 2)
    add_block(block_of(0, 2, core))
    pass_on(0, 3, 1)
    pass_on(0, 3, 3)
    add_sibling(0, 1)
    pass_on(1, 0, 1, [(right, 1), (left, 2)])
    add_sibling(0, 2)
    pass_on(1, 1, 0, [(right, 3)])
    pass_on(1, 2, 0)
    add_block(block_of(0, 3, core))
    pass_on(1, 1, 2)
    pass_on(1, 2, 2, [(left, 3)])
    pass_on(1, 0, 3, [(left, 2), (right, 1)])
    add_sibling(0, 3)
    pass_on(1, 1, 1, [(right, 3)])
    pass_on(1, 2, 1)
    add_block(block_of(1, 0, core))
    pass_on(1, 3, 0)
    pass_on(1, 3, 2)
    add_sibling(1, 0)
    pass_on(1, 2, 3, [(left, 3)])
    pass_on(1, 1, 3)
    add_block(block_of(1, 1, core))
    add_block(block_of(1, 2, core))
    pass_on(1, 3, 1)
    pass_on(1, 3, 3)
    add_sibling(1, 1)
    add_sibling(1, 2)
    add_block(block_of(1, 3, core))
    add_sibling(1, 3)

    def send_rows(step, carry):
        other = lax.rem(row + step, ROWS)
        pltpu.make_async_remote_copy(
            src_ref=total.at[pl.ds(pl.multiple_of(other * NOUT, NOUT), NOUT)], dst_ref=rbuf.at[row],
            send_sem=r_send.at[0], recv_sem=r_recv.at[0], device_id=(other, col), device_id_type=MESH,
        ).start()
        return carry

    lax.fori_loop(1, ROWS, send_rows, 0)
    rbuf[row] = total[pl.ds(pl.multiple_of(row * NOUT, NOUT), NOUT), :]
    at_row = lax.broadcasted_iota(jnp.int32, (NOUT, NPAIR), 0)
    window = jnp.zeros((NOUT, NPAIR), jnp.float32)
    for n in range(NOUT):
        window = jnp.where(at_row == n, pair_e[n], window)
    denominator = window - e_first - e_second
    peers = rbuf.at[pl.ds(0, ROWS - 1)]
    pltpu.make_async_copy(peers, peers, r_recv.at[0]).wait()
    ladder = rbuf[0]
    for r in range(1, ROWS):
        ladder = ladder + rbuf[r]
    out_ref[...] = (ladder / denominator).astype(jnp.bfloat16)

    for copy in started + sib_started:
        copy.wait_send()
    pltpu.make_async_copy(others, others, s_send.at[0]).wait()
    plane_copy.wait_send()
    pltpu.make_async_copy(peers, peers, r_send.at[0]).wait()


def body(amplitudes, singles, integrals, occ_energy, pair_energy, occ_irrep, virt_irrep, pair_list):
    hbm = pl.BlockSpec(memory_space=pltpu.MemorySpace.HBM)
    vmem = pl.BlockSpec(memory_space=pltpu.VMEM)
    dma = pltpu.SemaphoreType.DMA
    return pl.pallas_call(
        kernel,
        out_shape=jax.ShapeDtypeStruct((NOUT, NPAIR), jnp.bfloat16),
        in_specs=[hbm] * 8,
        out_specs=vmem,
        scratch_shapes=[
            pltpu.VMEM((1, NOCC), jnp.float32),
            pltpu.SMEM((NOUT,), jnp.float32),
            pltpu.VMEM((1, NOCC), jnp.int32),
            pltpu.VMEM((NVIRT,), jnp.int32),
            pltpu.SMEM((NVIRT,), jnp.int32),
            pltpu.VMEM((2, COLS * NPAIR), jnp.int32),
            pltpu.VMEM((CB, NVIRT, NPAIR), jnp.bfloat16),
            pltpu.VMEM((CORES, PLANE, DB, NOCC), jnp.bfloat16),
            pltpu.VMEM((COLS, KB, NWIN), jnp.bfloat16),
            pltpu.VMEM((COLS, KB, NPAIR), jnp.bfloat16),
            pltpu.VMEM((NVIRT, NPAIR), jnp.int32),
            pltpu.VMEM((NVIRT, NPAIR), jnp.float32),
            pltpu.VMEM((NVIRT, NPAIR), jnp.float32),
            pltpu.VMEM((NWIN, NPAIR), jnp.float32),
            pltpu.VMEM((ROWS, NOUT, NPAIR), jnp.float32),
            dma((9,)),
            dma((2,)),
            dma((2,)),
            dma((28,)),
            dma((32,)),
            dma((32,)),
            dma((32,)),
            dma((1,)),
            dma((1,)),
        ],
        compiler_params=pltpu.CompilerParams(
            collective_id=0, has_side_effects=True, vmem_limit_bytes=67043328
        ),
        name="ladder",
    )(
        amplitudes,
        singles,
        integrals.reshape(KB, NWIN),
        occ_energy.reshape(1, NOCC),
        pair_energy,
        occ_irrep.reshape(1, NOCC),
        virt_irrep,
        pair_list.T,
    )


def solution(mesh):
    return jax.shard_map(
        body,
        mesh=mesh,
        in_specs=(
            P("row", None, "col"),
            P("col", None),
            P("row", "col", None),
            P(),
            P("row"),
            P(),
            P(),
            P(),
        ),
        out_specs=P("row", "col"),
        check_vma=False,
    )
```

```python
import functools

import jax
import jax.numpy as jnp
from jax import lax
from jax.experimental import pallas as pl
from jax.experimental.pallas import tpu as pltpu
from jax.sharding import PartitionSpec as P

MESH = pl.DeviceIdType.MESH
NX = 4
ROWS = 32
COLS = 16
CORES = 2

CB = 20
DB = 40
KB = CB * DB
PIECES = ((0, 208), (208, 192), (400, 208), (608, 192))
NZ = 8
NY = 4
PLANE = 8
NVIRT = 640
NOCC = 200
NPAIR = 128
NWIN = 256
NOUT = 8


def contract(a, b):
    return lax.dot_general(a, b, (((0,), (0,)), ((), ())), preferred_element_type=jnp.float32)


def kernel(
    amp_hbm, singles_hbm, integ_hbm, occ_e_hbm, pair_e_hbm, occ_l_hbm, virt_hbm, pairs_hbm, out_ref,
    occ_e, pair_e, occ_l, virt_row, virt_l, pairs, amp, sblk, ibuf, tau, labels, d_val, c_val, total, rbuf,
    local_sem, s_send, s_recv, send_sem, recv_sem, sib_send, sib_recv, r_send, r_recv, rounds,
):
    row = lax.axis_index("row")
    col = lax.axis_index("col")
    core = lax.rem(col, CORES)
    xat = lax.rem(col // CORES, NX)
    yhi = col // (CORES * NX)

    def col_of(y, x, k):
        return y * (CORES * NX) + x * CORES + k

    right = col_of(yhi, lax.rem(xat + 1, NX), core)
    left = col_of(yhi, lax.rem(xat + NX - 1, NX), core)
    across = col_of(1 - yhi, xat, core)
    sibling = col_of(yhi, xat, 1 - core)

    amp_copy = pltpu.make_async_copy(amp_hbm, amp, local_sem.at[0])
    amp_copy.start()
    own_copy = pltpu.make_async_copy(integ_hbm, ibuf.at[col], local_sem.at[1])
    own_copy.start()
    spot = col // CORES
    s_copy = pltpu.make_async_copy(singles_hbm, sblk.at[core, spot], local_sem.at[2])
    s_copy.start()

    small_copies = []
    for n, (src, dst) in enumerate(
        (
            (pairs_hbm, pairs),
            (occ_e_hbm, occ_e),
            (occ_l_hbm, occ_l),
            (virt_hbm, virt_row),
            (virt_hbm, virt_l),
            (pair_e_hbm, pair_e),
        )
    ):
        copy = pltpu.make_async_copy(src, dst, local_sem.at[3 + n])
        copy.start()
        small_copies.append(copy)

    barrier = pltpu.get_barrier_semaphore()

    zat, yat = lax.rem(row, NZ), row // NZ

    def row_at(y, z):
        return lax.rem(y + NY, NY) * NZ + lax.rem(z + NZ, NZ)

    z_near = (row_at(yat, zat + 1), row_at(yat, zat - 1))
    z_far = (row_at(yat, zat + 2), row_at(yat, zat - 2))
    y_near = row_at(yat + 1 - 2 * lax.rem(yat, 2), zat)
    y_far = row_at(yat + 2, zat)

    def tell(semaphore, targets):
        for other in targets:
            pl.semaphore_signal(semaphore, inc=1, device_id=(other, col), device_id_type=MESH)

    def greet_plane(step, carry):
        other = lax.rem(spot + step, PLANE) * CORES + core
        pl.semaphore_signal(barrier, inc=1, device_id=(row, other), device_id_type=MESH)
        return carry

    pl.semaphore_signal(barrier, inc=1, device_id=(row, sibling), device_id_type=MESH)
    lax.fori_loop(1, PLANE, greet_plane, 0)
    tell(barrier, z_near + (y_near, y_far))
    pl.semaphore_wait(barrier, PLANE + 4)

    def send_single(step, carry):
        other = lax.rem(spot + step, PLANE) * CORES + core
        pltpu.make_async_remote_copy(
            src_ref=singles_hbm, dst_ref=sblk.at[core, spot], send_sem=s_send.at[0], recv_sem=s_recv.at[0],
            device_id=(row, other), device_id_type=MESH,
        ).start()
        return carry

    lax.fori_loop(1, PLANE, send_single, 0)

    started = []

    def half(at, h):
        return ibuf.at[at, pl.ds(*PIECES[h])]

    def push(src, at, h, target, slot):
        copy = pltpu.make_async_remote_copy(
            src_ref=src, dst_ref=half(at, h), send_sem=send_sem.at[len(started)], recv_sem=recv_sem.at[slot],
            device_id=(row, target), device_id_type=MESH,
        )
        copy.start()
        started.append(copy)

    def to_sibling(src, at, h, slot):
        copy = pltpu.make_async_remote_copy(
            src_ref=src, dst_ref=half(at, h), send_sem=sib_send.at[slot], recv_sem=sib_recv.at[slot],
            device_id=(row, sibling), device_id_type=MESH,
        )
        copy.start()
        sib_started.append(copy)

    sib_started = []

    def arrived(at, h, slot):
        ref = half(at, h)
        pltpu.make_async_copy(ref, ref, recv_sem.at[slot]).wait()

    def sib_arrived(at, h, slot):
        ref = half(at, h)
        pltpu.make_async_copy(ref, ref, sib_recv.at[slot]).wait()

    def slot_of(s, q, h):
        return (s * 4 + q) * len(PIECES) + h

    def block_of(s, q, k):
        y = yhi if s == 0 else 1 - yhi
        x = lax.rem(xat + (0, NX - 1, 1, 2)[q], NX)
        return col_of(y, x, k)

    def own_half(h):
        return integ_hbm.at[pl.ds(*PIECES[h])]

    for to_right, to_left, to_across in ((0, 2, 0), (1, 3, 2), (2, 0, 1), (3, 1, 3)):
        push(own_half(to_across), col, to_across, across, slot_of(1, 0, to_across))
        push(own_half(to_right), col, to_right, right, slot_of(0, 1, to_right))
        push(own_half(to_left), col, to_left, left, slot_of(0, 2, to_left))
    for h in range(len(PIECES)):
        to_sibling(own_half(h), col, h, slot_of(0, 0, h))

    tell(rounds.at[0], z_near)

    for copy in small_copies:
        copy.wait()
    first = pairs[0:1, pl.ds(pl.multiple_of(col * NPAIR, NPAIR), NPAIR)]
    second = pairs[1:2, pl.ds(pl.multiple_of(col * NPAIR, NPAIR), NPAIR)]
    both = jnp.concatenate([second, first], axis=1)
    orbital = lax.broadcasted_iota(jnp.int32, (NOCC, 2 * NPAIR), 0)
    pick = jnp.where(orbital == both, 1.0, 0.0).astype(jnp.bfloat16)

    energy = occ_e[...]
    part_a = energy.astype(jnp.bfloat16).astype(jnp.float32)
    part_b = (energy - part_a).astype(jnp.bfloat16).astype(jnp.float32)
    part_c = energy - part_a - part_b
    place = lax.broadcasted_iota(jnp.int32, (16, NOCC), 0)
    table = jnp.where(place == 0, part_a, jnp.where(place == 1, part_b, jnp.where(place == 2, part_c, 0.0)))
    table = jnp.where(place == 3, occ_l[...].astype(jnp.float32), table).astype(jnp.bfloat16)
    found = jnp.dot(table, pick, preferred_element_type=jnp.float32)
    occ_pair = found[0:1] + found[1:2] + found[2:3]
    label_pair = found[3:4].astype(jnp.int32)
    e_second, e_first = occ_pair[:, :NPAIR], occ_pair[:, NPAIR:]
    sym = jnp.bitwise_xor(label_pair[:, :NPAIR], label_pair[:, NPAIR:])
    virt = jnp.broadcast_to(virt_row[...].reshape(1, NVIRT).astype(jnp.float32), (NPAIR, NVIRT)).T
    labels[...] = jnp.bitwise_xor(virt.astype(jnp.int32), sym)
    total[...] = jnp.zeros_like(total)

    def add_block(at):
        total[...] += contract(ibuf[at], tau[at])

    def add_piece(at, h):
        rows = pl.ds(*PIECES[h])
        total[...] += contract(ibuf[at, rows], tau[at, rows])

    def add_sibling_piece(s, q, h):
        at = block_of(s, q, 1 - core)
        sib_arrived(at, h, slot_of(s, q, h))
        add_piece(at, h)

    def pass_on(s, q, h, onward=()):
        at = block_of(s, q, core)
        arrived(at, h, slot_of(s, q, h))
        for target, q_there in onward:
            push(half(at, h), at, h, target, slot_of(s, q_there, h))
        to_sibling(half(at, h), at, h, slot_of(s, q, h))

    def add_sibling(s, q):
        at = block_of(s, q, 1 - core)
        for h in range(len(PIECES)):
            sib_arrived(at, h, slot_of(s, q, h))
        add_block(at)

    pass_on(0, 1, 0, [(right, 3)])
    pass_on(0, 2, 2, [(left, 3)])
    pl.semaphore_wait(rounds.at[0], 2)
    tell(rounds.at[1], z_far)

    s_copy.wait()
    others = sblk.at[0, pl.ds(0, PLANE - 1)]
    pltpu.make_async_copy(others, others, s_recv.at[0]).wait()
    plane_copy = pltpu.make_async_remote_copy(
        src_ref=sblk.at[core], dst_ref=sblk.at[core], send_sem=s_send.at[1], recv_sem=s_recv.at[1],
        device_id=(row, sibling), device_id_type=MESH,
    )
    plane_copy.start()
    pass_on(0, 1, 1, [(right, 3)])
    pass_on(0, 2, 3, [(left, 3)])
    pl.semaphore_wait(rounds.at[1], 2)
    tell(rounds.at[2], (y_near,))
    plane_copy.wait_recv()
    for b in range(COLS):
        at_pairs = jnp.dot(sblk[b % CORES, b // CORES], pick, preferred_element_type=jnp.float32)
        d_val[pl.ds(b * DB, DB), :] = at_pairs[:, :NPAIR]
        c_val[pl.ds(b * DB, DB), :] = at_pairs[:, NPAIR:]
    amp_copy.wait()

    def tau_step(m, carry):
        d_at = pl.multiple_of(m * (2 * DB), 2 * DB)
        d_lab = labels[pl.ds(d_at, 2 * DB), :]
        d_one = d_val[pl.ds(d_at, 2 * DB), :]

        def tau_pair(c2, carry):
            vals = []
            for u in range(2):
                c = c2 * 2 + u
                c_one = c_val[pl.ds(row * CB + c, 1), :]
                val = amp[c, pl.ds(d_at, 2 * DB), :].astype(jnp.float32) + c_one * d_one
                vals.append(jnp.where(d_lab == virt_l[row * CB + c], val, 0.0))
            k_at = pl.multiple_of(c2 * (2 * DB), 2 * DB)
            for v in range(2):
                rows = jnp.concatenate([val[v * DB : (v + 1) * DB] for val in vals], axis=0)
                tau[m * 2 + v, pl.ds(k_at, 2 * DB), :] = rows.astype(jnp.bfloat16)
            return carry

        return lax.fori_loop(0, CB // 2, tau_pair, carry)

    lax.fori_loop(0, COLS // 2, tau_step, 0)

    pass_on(1, 0, 0, [(right, 1), (left, 2)])
    pl.semaphore_wait(rounds.at[2], 1)
    tell(rounds.at[3], (y_far,))
    pass_on(0, 1, 2)
    pass_on(0, 2, 0)
    own_copy.wait()
    add_block(col)
    pass_on(0, 1, 3)
    pass_on(0, 2, 1)
    pass_on(1, 0, 2, [(left, 2), (right, 1)])
    add_sibling(0, 0)
    add_block(block_of(0, 1, core))
    pass_on(0, 3, 0)
    pass_on(0, 3, 2)
    add_block(block_of(0, 2, core))
    pass_on(0, 3, 1)
    pass_on(0, 3, 3)
    add_sibling(0, 1)
    pass_on(1, 0, 1, [(right, 1), (left, 2)])
    add_sibling(0, 2)
    pass_on(1, 1, 0, [(right, 3)])
    pass_on(1, 2, 0)
    add_block(block_of(0, 3, core))
    pass_on(1, 1, 2)
    pass_on(1, 2, 2, [(left, 3)])
    pass_on(1, 0, 3, [(left, 2), (right, 1)])
    add_sibling(0, 3)
    pass_on(1, 1, 1, [(right, 3)])
    pass_on(1, 2, 1)
    add_block(block_of(1, 0, core))
    pass_on(1, 3, 0)
    pass_on(1, 3, 2)
    add_sibling(1, 0)
    pass_on(1, 2, 3, [(left, 3)])
    pass_on(1, 1, 3)
    last = block_of(1, 3, core)
    add_block(block_of(1, 1, core))
    add_block(block_of(1, 2, core))
    add_piece(last, 0)
    add_piece(last, 2)
    pass_on(1, 3, 1)
    add_sibling(1, 1)
    add_piece(last, 1)
    pass_on(1, 3, 3)
    add_sibling(1, 2)
    add_piece(last, 3)
    for h in (0, 2, 1, 3):
        add_sibling_piece(1, 3, h)

    def send_rows(step, carry):
        other = lax.rem(row + step, ROWS)
        pltpu.make_async_remote_copy(
            src_ref=total.at[pl.ds(pl.multiple_of(other * NOUT, NOUT), NOUT)], dst_ref=rbuf.at[row],
            send_sem=r_send.at[0], recv_sem=r_recv.at[0], device_id=(other, col), device_id_type=MESH,
        ).start()
        return carry

    pl.semaphore_wait(rounds.at[3], 1)
    lax.fori_loop(1, ROWS, send_rows, 0)
    rbuf[row] = total[pl.ds(pl.multiple_of(row * NOUT, NOUT), NOUT), :]
    at_row = lax.broadcasted_iota(jnp.int32, (NOUT, NPAIR), 0)
    window = jnp.zeros((NOUT, NPAIR), jnp.float32)
    for n in range(NOUT):
        window = jnp.where(at_row == n, pair_e[n], window)
    denominator = window - e_first - e_second
    peers = rbuf.at[pl.ds(0, ROWS - 1)]
    pltpu.make_async_copy(peers, peers, r_recv.at[0]).wait()
    ladder = rbuf[0]
    for r in range(1, ROWS):
        ladder = ladder + rbuf[r]
    out_ref[...] = (ladder / denominator).astype(jnp.bfloat16)

    for copy in started + sib_started:
        copy.wait_send()
    pltpu.make_async_copy(others, others, s_send.at[0]).wait()
    plane_copy.wait_send()
    pltpu.make_async_copy(peers, peers, r_send.at[0]).wait()


def body(amplitudes, singles, integrals, occ_energy, pair_energy, occ_irrep, virt_irrep, pair_list):
    hbm = pl.BlockSpec(memory_space=pltpu.MemorySpace.HBM)
    vmem = pl.BlockSpec(memory_space=pltpu.VMEM)
    dma = pltpu.SemaphoreType.DMA
    return pl.pallas_call(
        kernel,
        out_shape=jax.ShapeDtypeStruct((NOUT, NPAIR), jnp.bfloat16),
        in_specs=[hbm] * 8,
        out_specs=vmem,
        scratch_shapes=[
            pltpu.VMEM((1, NOCC), jnp.float32),
            pltpu.SMEM((NOUT,), jnp.float32),
            pltpu.VMEM((1, NOCC), jnp.int32),
            pltpu.VMEM((NVIRT,), jnp.int32),
            pltpu.SMEM((NVIRT,), jnp.int32),
            pltpu.VMEM((2, COLS * NPAIR), jnp.int32),
            pltpu.VMEM((CB, NVIRT, NPAIR), jnp.bfloat16),
            pltpu.VMEM((CORES, PLANE, DB, NOCC), jnp.bfloat16),
            pltpu.VMEM((COLS, KB, NWIN), jnp.bfloat16),
            pltpu.VMEM((COLS, KB, NPAIR), jnp.bfloat16),
            pltpu.VMEM((NVIRT, NPAIR), jnp.int32),
            pltpu.VMEM((NVIRT, NPAIR), jnp.float32),
            pltpu.VMEM((NVIRT, NPAIR), jnp.float32),
            pltpu.VMEM((NWIN, NPAIR), jnp.float32),
            pltpu.VMEM((ROWS, NOUT, NPAIR), jnp.float32),
            dma((9,)),
            dma((2,)),
            dma((2,)),
            dma((28,)),
            dma((32,)),
            dma((32,)),
            dma((32,)),
            dma((1,)),
            dma((1,)),
            pltpu.SemaphoreType.REGULAR((4,)),
        ],
        compiler_params=pltpu.CompilerParams(
            collective_id=0, has_side_effects=True, vmem_limit_bytes=67043328
        ),
        name="ladder",
    )(
        amplitudes,
        singles,
        integrals.reshape(KB, NWIN),
        occ_energy.reshape(1, NOCC),
        pair_energy,
        occ_irrep.reshape(1, NOCC),
        virt_irrep,
        pair_list.T,
    )


def solution(mesh):
    return jax.shard_map(
        body,
        mesh=mesh,
        in_specs=(
            P("row", None, "col"),
            P("col", None),
            P("row", "col", None),
            P(),
            P("row"),
            P(),
            P(),
            P(),
        ),
        out_specs=P("row", "col"),
        check_vma=False,
    )
```

```python
import functools

import jax
import jax.numpy as jnp
from jax import lax
from jax.experimental import pallas as pl
from jax.experimental.pallas import tpu as pltpu
from jax.sharding import PartitionSpec as P

MESH = pl.DeviceIdType.MESH
NX = 4
ROWS = 32
COLS = 16
CORES = 2

CB = 20
DB = 40
KB = CB * DB
PIECES = ((0, 208), (208, 192), (400, 208), (608, 192))
NZ = 8
NY = 4
PLANE = 8
NVIRT = 640
NOCC = 200
NPAIR = 128
NWIN = 256
NOUT = 8


def contract(a, b):
    return lax.dot_general(a, b, (((0,), (0,)), ((), ())), preferred_element_type=jnp.float32)


def kernel(
    amp_hbm, singles_hbm, integ_hbm, occ_e_hbm, pair_e_hbm, occ_l_hbm, virt_hbm, pairs_hbm, out_ref,
    occ_e, pair_e, occ_l, virt_row, virt_l, pairs, amp, sblk, ibuf, tau, labels, d_val, c_val, total, rbuf,
    local_sem, s_send, s_recv, send_sem, recv_sem, sib_send, sib_recv, r_send, r_recv, rounds,
):
    row = lax.axis_index("row")
    col = lax.axis_index("col")
    core = lax.rem(col, CORES)
    xat = lax.rem(col // CORES, NX)
    yhi = col // (CORES * NX)

    def col_of(y, x, k):
        return y * (CORES * NX) + x * CORES + k

    right = col_of(yhi, lax.rem(xat + 1, NX), core)
    left = col_of(yhi, lax.rem(xat + NX - 1, NX), core)
    across = col_of(1 - yhi, xat, core)
    sibling = col_of(yhi, xat, 1 - core)

    amp_copy = pltpu.make_async_copy(amp_hbm, amp, local_sem.at[0])
    amp_copy.start()
    own_copy = pltpu.make_async_copy(integ_hbm, ibuf.at[col], local_sem.at[1])
    own_copy.start()
    spot = col // CORES
    s_copy = pltpu.make_async_copy(singles_hbm, sblk.at[core, spot], local_sem.at[2])
    s_copy.start()

    small_copies = []
    for n, (src, dst) in enumerate(
        (
            (pairs_hbm, pairs),
            (occ_e_hbm, occ_e),
            (occ_l_hbm, occ_l),
            (virt_hbm, virt_row),
            (virt_hbm, virt_l),
            (pair_e_hbm, pair_e),
        )
    ):
        copy = pltpu.make_async_copy(src, dst, local_sem.at[3 + n])
        copy.start()
        small_copies.append(copy)

    barrier = pltpu.get_barrier_semaphore()

    zat, yat = lax.rem(row, NZ), row // NZ

    def row_at(y, z):
        return lax.rem(y + NY, NY) * NZ + lax.rem(z + NZ, NZ)

    z_near = (row_at(yat, zat + 1), row_at(yat, zat - 1))
    z_far = (row_at(yat, zat + 2), row_at(yat, zat - 2))
    y_near = row_at(yat + 1 - 2 * lax.rem(yat, 2), zat)
    y_far = row_at(yat + 2, zat)

    def tell(semaphore, targets):
        for other in targets:
            pl.semaphore_signal(semaphore, inc=1, device_id=(other, col), device_id_type=MESH)

    def greet_plane(step, carry):
        other = lax.rem(spot + step, PLANE) * CORES + core
        pl.semaphore_signal(barrier, inc=1, device_id=(row, other), device_id_type=MESH)
        return carry

    pl.semaphore_signal(barrier, inc=1, device_id=(row, sibling), device_id_type=MESH)
    lax.fori_loop(1, PLANE, greet_plane, 0)
    tell(barrier, z_near + (y_near, y_far))
    pl.semaphore_wait(barrier, PLANE + 4)

    def send_single(step, carry):
        other = lax.rem(spot + step, PLANE) * CORES + core
        pltpu.make_async_remote_copy(
            src_ref=singles_hbm, dst_ref=sblk.at[core, spot], send_sem=s_send.at[0], recv_sem=s_recv.at[0],
            device_id=(row, other), device_id_type=MESH,
        ).start()
        return carry

    lax.fori_loop(1, PLANE, send_single, 0)

    started = []

    def half(at, h):
        return ibuf.at[at, pl.ds(*PIECES[h])]

    def push(src, at, h, target, slot):
        copy = pltpu.make_async_remote_copy(
            src_ref=src, dst_ref=half(at, h), send_sem=send_sem.at[len(started)], recv_sem=recv_sem.at[slot],
            device_id=(row, target), device_id_type=MESH,
        )
        copy.start()
        started.append(copy)

    def to_sibling(src, at, h, slot):
        copy = pltpu.make_async_remote_copy(
            src_ref=src, dst_ref=half(at, h), send_sem=sib_send.at[slot], recv_sem=sib_recv.at[slot],
            device_id=(row, sibling), device_id_type=MESH,
        )
        copy.start()
        sib_started.append(copy)

    sib_started = []

    def arrived(at, h, slot):
        ref = half(at, h)
        pltpu.make_async_copy(ref, ref, recv_sem.at[slot]).wait()

    def sib_arrived(at, h, slot):
        ref = half(at, h)
        pltpu.make_async_copy(ref, ref, sib_recv.at[slot]).wait()

    def slot_of(s, q, h):
        return (s * 4 + q) * len(PIECES) + h

    def block_of(s, q, k):
        y = yhi if s == 0 else 1 - yhi
        x = lax.rem(xat + (0, NX - 1, 1, 2)[q], NX)
        return col_of(y, x, k)

    def own_half(h):
        return integ_hbm.at[pl.ds(*PIECES[h])]

    for to_right, to_left, to_across in ((0, 2, 0), (1, 3, 2), (2, 0, 1), (3, 1, 3)):
        push(own_half(to_across), col, to_across, across, slot_of(1, 0, to_across))
        push(own_half(to_right), col, to_right, right, slot_of(0, 1, to_right))
        push(own_half(to_left), col, to_left, left, slot_of(0, 2, to_left))
    for h in range(len(PIECES)):
        to_sibling(own_half(h), col, h, slot_of(0, 0, h))

    tell(rounds.at[0], z_near)

    for copy in small_copies:
        copy.wait()
    first = pairs[0:1, pl.ds(pl.multiple_of(col * NPAIR, NPAIR), NPAIR)]
    second = pairs[1:2, pl.ds(pl.multiple_of(col * NPAIR, NPAIR), NPAIR)]
    both = jnp.concatenate([second, first], axis=1)
    orbital = lax.broadcasted_iota(jnp.int32, (NOCC, 2 * NPAIR), 0)
    pick = jnp.where(orbital == both, 1.0, 0.0).astype(jnp.bfloat16)

    energy = occ_e[...]
    part_a = energy.astype(jnp.bfloat16).astype(jnp.float32)
    part_b = (energy - part_a).astype(jnp.bfloat16).astype(jnp.float32)
    part_c = energy - part_a - part_b
    place = lax.broadcasted_iota(jnp.int32, (16, NOCC), 0)
    table = jnp.where(place == 0, part_a, jnp.where(place == 1, part_b, jnp.where(place == 2, part_c, 0.0)))
    table = jnp.where(place == 3, occ_l[...].astype(jnp.float32), table).astype(jnp.bfloat16)
    found = jnp.dot(table, pick, preferred_element_type=jnp.float32)
    occ_pair = found[0:1] + found[1:2] + found[2:3]
    label_pair = found[3:4].astype(jnp.int32)
    e_second, e_first = occ_pair[:, :NPAIR], occ_pair[:, NPAIR:]
    sym = jnp.bitwise_xor(label_pair[:, :NPAIR], label_pair[:, NPAIR:])
    virt = jnp.broadcast_to(virt_row[...].reshape(1, NVIRT).astype(jnp.float32), (NPAIR, NVIRT)).T
    labels[...] = jnp.bitwise_xor(virt.astype(jnp.int32), sym)
    total[...] = jnp.zeros_like(total)

    def add_block(at):
        total[...] += contract(ibuf[at], tau[at])

    def add_piece(at, h):
        rows = pl.ds(*PIECES[h])
        total[...] += contract(ibuf[at, rows], tau[at, rows])

    def add_sibling_piece(s, q, h):
        at = block_of(s, q, 1 - core)
        sib_arrived(at, h, slot_of(s, q, h))
        add_piece(at, h)

    def pass_on(s, q, h, onward=()):
        at = block_of(s, q, core)
        arrived(at, h, slot_of(s, q, h))
        for target, q_there in onward:
            push(half(at, h), at, h, target, slot_of(s, q_there, h))
        to_sibling(half(at, h), at, h, slot_of(s, q, h))

    def add_sibling(s, q):
        at = block_of(s, q, 1 - core)
        for h in range(len(PIECES)):
            sib_arrived(at, h, slot_of(s, q, h))
        add_block(at)

    pass_on(0, 1, 0, [(right, 3)])
    pass_on(0, 2, 2, [(left, 3)])
    pl.semaphore_wait(rounds.at[0], 2)
    tell(rounds.at[1], z_far)

    s_copy.wait()
    others = sblk.at[0, pl.ds(0, PLANE - 1)]
    pltpu.make_async_copy(others, others, s_recv.at[0]).wait()
    plane_copy = pltpu.make_async_remote_copy(
        src_ref=sblk.at[core], dst_ref=sblk.at[core], send_sem=s_send.at[1], recv_sem=s_recv.at[1],
        device_id=(row, sibling), device_id_type=MESH,
    )
    plane_copy.start()
    pass_on(0, 1, 1, [(right, 3)])
    pass_on(0, 2, 3, [(left, 3)])
    pl.semaphore_wait(rounds.at[1], 2)
    tell(rounds.at[2], (y_near,))
    plane_copy.wait_recv()
    for b in range(COLS):
        at_pairs = jnp.dot(sblk[b % CORES, b // CORES], pick, preferred_element_type=jnp.float32)
        d_val[pl.ds(b * DB, DB), :] = at_pairs[:, :NPAIR]
        c_val[pl.ds(b * DB, DB), :] = at_pairs[:, NPAIR:]
    amp_copy.wait()

    def tau_step(m, carry):
        d_at = pl.multiple_of(m * (2 * DB), 2 * DB)
        d_lab = labels[pl.ds(d_at, 2 * DB), :]
        d_one = d_val[pl.ds(d_at, 2 * DB), :]

        def tau_pair(c2, carry):
            vals = []
            for u in range(2):
                c = c2 * 2 + u
                c_one = c_val[pl.ds(row * CB + c, 1), :]
                val = amp[c, pl.ds(d_at, 2 * DB), :].astype(jnp.float32) + c_one * d_one
                vals.append(jnp.where(d_lab == virt_l[row * CB + c], val, 0.0))
            k_at = pl.multiple_of(c2 * (2 * DB), 2 * DB)
            for v in range(2):
                rows = jnp.concatenate([val[v * DB : (v + 1) * DB] for val in vals], axis=0)
                tau[m * 2 + v, pl.ds(k_at, 2 * DB), :] = rows.astype(jnp.bfloat16)
            return carry

        return lax.fori_loop(0, CB // 2, tau_pair, carry)

    lax.fori_loop(0, COLS // 2, tau_step, 0)

    pass_on(1, 0, 0, [(right, 1), (left, 2)])
    pl.semaphore_wait(rounds.at[2], 1)
    tell(rounds.at[3], (y_far,))
    pass_on(0, 1, 2)
    pass_on(0, 2, 0)
    own_copy.wait()
    add_block(col)
    pass_on(0, 1, 3)
    pass_on(0, 2, 1)
    pass_on(1, 0, 2, [(left, 2), (right, 1)])
    add_sibling(0, 0)
    add_block(block_of(0, 1, core))
    pass_on(0, 3, 0)
    pass_on(0, 3, 2)
    add_block(block_of(0, 2, core))
    pass_on(0, 3, 1)
    pass_on(0, 3, 3)
    add_sibling(0, 1)
    pass_on(1, 0, 1, [(right, 1), (left, 2)])
    add_sibling(0, 2)
    pass_on(1, 1, 0, [(right, 3)])
    pass_on(1, 2, 0)
    add_block(block_of(0, 3, core))
    pass_on(1, 1, 2)
    pass_on(1, 2, 2, [(left, 3)])
    pass_on(1, 0, 3, [(left, 2), (right, 1)])
    add_sibling(0, 3)
    pass_on(1, 1, 1, [(right, 3)])
    pass_on(1, 2, 1)
    add_block(block_of(1, 0, core))
    pass_on(1, 3, 0)
    pass_on(1, 3, 2)
    add_sibling(1, 0)
    pass_on(1, 2, 3, [(left, 3)])
    pass_on(1, 1, 3)
    last = block_of(1, 3, core)
    add_block(block_of(1, 1, core))
    add_block(block_of(1, 2, core))
    add_piece(last, 0)
    add_piece(last, 2)
    pass_on(1, 3, 1)
    add_sibling(1, 1)
    add_piece(last, 1)
    pass_on(1, 3, 3)
    add_sibling(1, 2)
    add_piece(last, 3)
    for h in (0, 2, 1, 3):
        add_sibling_piece(1, 3, h)

    pl.semaphore_wait(rounds.at[3], 1)
    for z_step in (4, 3, 5, 2, 6, 1, 7, 0):
        for y_step in (3, 1, 2, 0):
            if z_step == 0 and y_step == 0:
                continue
            other = row_at(yat + y_step, zat + z_step)
            pltpu.make_async_remote_copy(
                src_ref=total.at[pl.ds(pl.multiple_of(other * NOUT, NOUT), NOUT)], dst_ref=rbuf.at[row],
                send_sem=r_send.at[0], recv_sem=r_recv.at[0], device_id=(other, col), device_id_type=MESH,
            ).start()
    rbuf[row] = total[pl.ds(pl.multiple_of(row * NOUT, NOUT), NOUT), :]
    at_row = lax.broadcasted_iota(jnp.int32, (NOUT, NPAIR), 0)
    window = jnp.zeros((NOUT, NPAIR), jnp.float32)
    for n in range(NOUT):
        window = jnp.where(at_row == n, pair_e[n], window)
    denominator = window - e_first - e_second
    peers = rbuf.at[pl.ds(0, ROWS - 1)]
    pltpu.make_async_copy(peers, peers, r_recv.at[0]).wait()
    ladder = rbuf[0]
    for r in range(1, ROWS):
        ladder = ladder + rbuf[r]
    out_ref[...] = (ladder / denominator).astype(jnp.bfloat16)

    for copy in started + sib_started:
        copy.wait_send()
    pltpu.make_async_copy(others, others, s_send.at[0]).wait()
    plane_copy.wait_send()
    pltpu.make_async_copy(peers, peers, r_send.at[0]).wait()


def body(amplitudes, singles, integrals, occ_energy, pair_energy, occ_irrep, virt_irrep, pair_list):
    hbm = pl.BlockSpec(memory_space=pltpu.MemorySpace.HBM)
    vmem = pl.BlockSpec(memory_space=pltpu.VMEM)
    dma = pltpu.SemaphoreType.DMA
    return pl.pallas_call(
        kernel,
        out_shape=jax.ShapeDtypeStruct((NOUT, NPAIR), jnp.bfloat16),
        in_specs=[hbm] * 8,
        out_specs=vmem,
        scratch_shapes=[
            pltpu.VMEM((1, NOCC), jnp.float32),
            pltpu.SMEM((NOUT,), jnp.float32),
            pltpu.VMEM((1, NOCC), jnp.int32),
            pltpu.VMEM((NVIRT,), jnp.int32),
            pltpu.SMEM((NVIRT,), jnp.int32),
            pltpu.VMEM((2, COLS * NPAIR), jnp.int32),
            pltpu.VMEM((CB, NVIRT, NPAIR), jnp.bfloat16),
            pltpu.VMEM((CORES, PLANE, DB, NOCC), jnp.bfloat16),
            pltpu.VMEM((COLS, KB, NWIN), jnp.bfloat16),
            pltpu.VMEM((COLS, KB, NPAIR), jnp.bfloat16),
            pltpu.VMEM((NVIRT, NPAIR), jnp.int32),
            pltpu.VMEM((NVIRT, NPAIR), jnp.float32),
            pltpu.VMEM((NVIRT, NPAIR), jnp.float32),
            pltpu.VMEM((NWIN, NPAIR), jnp.float32),
            pltpu.VMEM((ROWS, NOUT, NPAIR), jnp.float32),
            dma((9,)),
            dma((2,)),
            dma((2,)),
            dma((28,)),
            dma((32,)),
            dma((32,)),
            dma((32,)),
            dma((1,)),
            dma((1,)),
            pltpu.SemaphoreType.REGULAR((4,)),
        ],
        compiler_params=pltpu.CompilerParams(
            collective_id=0, has_side_effects=True, vmem_limit_bytes=67043328
        ),
        name="ladder",
    )(
        amplitudes,
        singles,
        integrals.reshape(KB, NWIN),
        occ_energy.reshape(1, NOCC),
        pair_energy,
        occ_irrep.reshape(1, NOCC),
        virt_irrep,
        pair_list.T,
    )


def solution(mesh):
    return jax.shard_map(
        body,
        mesh=mesh,
        in_specs=(
            P("row", None, "col"),
            P("col", None),
            P("row", "col", None),
            P(),
            P("row"),
            P(),
            P(),
            P(),
        ),
        out_specs=P("row", "col"),
        check_vma=False,
    )
```
